32 devices in a mesh: row: 4 (over y, x), col: 4 (over z), depth: 2 (over core).
Axes of the slice: x: 2, y: 2, z: 4, core: 2. Of those that a mesh axis runs over, the one named last changes fastest.
Arguments:
- blocks: float32 [24, 4, 6, 128, 128], P('row', 'col'), may hold values from -1.2 to 1.2
- columns: int32 [24, 4, 6], P('row', 'col'), may hold values from 0 to 23, as said below
- branch: int32 [24], P('row'), may hold values 0 or 1
Outputs:
- updated: float32 [24, 4, 6, 128, 128], P('row', 'col')
- traces: float32 [2], replicated
The draws below stay inside these ranges and needn't reach their ends.
Inputs may be any that keep to these rules, and one draw needn't show every extreme that they name: Each block row names 6 distinct block columns in each column group g, all within g * 6 to (g + 1) * 6 - 1, and block row i names column i. `branch`: 1 selects the square for that block row, 0 selects 2 X minus the square.
All inputs are finite; a program needn't handle non-finite values.
Results may differ from the reference program's by a relative error of at most 0.0003.
Values sent between devices are 32-bit elements; how exact they have to be, the bound alone decides.
A program may use at most 64 MiB of HBM per device.

```python
import jax
import jax.numpy as jnp
from jax import lax

BS = 128
SPG = 6
CGROUPS = 4
NB = 24
COLGRP = 6


def draw_columns(key, part):
    key_list = jax.random.split(key, NB * CGROUPS)
    row_ids = jnp.repeat(jnp.arange(NB, dtype=jnp.int32), CGROUPS)
    group_ids = jnp.tile(jnp.arange(CGROUPS, dtype=jnp.int32), NB)

    def pick(single_key, row_id, group_id):
        shuffled = jax.random.permutation(single_key, COLGRP)
        placed = jnp.argsort(shuffled)
        local_ids = jnp.arange(COLGRP, dtype=jnp.int32)
        scores = jnp.where(local_ids + group_id * COLGRP == row_id, -1, placed)
        chosen = jnp.argsort(scores)[:SPG]
        return (chosen + group_id * COLGRP).astype(jnp.int32)
    return jax.vmap(pick)(key_list, row_ids, group_ids).reshape(NB, CGROUPS, SPG)


def touch_ends(array, own_key, smallest, top_value):
    spot = [jax.random.randint(jax.random.fold_in(own_key, axis), (), 0, length) for axis, length in enumerate(array.shape)]
    longest = array.shape.index(max(array.shape))
    next_to = spot[:longest] + [(spot[longest] + 1) % array.shape[longest]] + spot[longest + 1:]
    return array.at[tuple(spot)].set(smallest).at[tuple(next_to)].set(top_value)


def steps_of(rng, shape, pieces, smallest, largest):
    loudness = 1.0
    for axis_at, shards_of in pieces:
        steps = jax.random.uniform(jax.random.fold_in(jax.random.fold_in(rng, 6), axis_at), (shards_of,), jnp.float32, smallest / len(pieces), largest / len(pieces))
        loudness = loudness * jnp.repeat(jnp.exp(steps), shape[axis_at] // shards_of).reshape((-1,) + (1,) * (len(shape) - 1 - axis_at))
    return loudness


def noise(key, shape, width, reach, cuts=(), kind=jnp.bfloat16):
    loudness = steps_of(key, shape, cuts, -0.22, 0.18) if cuts else 1.0
    array = jax.random.normal(key, shape, jnp.float32) * width * loudness
    return jnp.minimum(jnp.maximum(array, -reach), reach).astype(kind)


def setup_inputs(seed: int = 0) -> dict:
    arg_keys = jax.random.split(jax.random.key(seed), 4)
    return {
        "blocks": noise(arg_keys[0], (NB, CGROUPS, SPG, BS, BS), 0.2, 1.2, ((0, 4), (1, 4)), jnp.float32),
        "columns": draw_columns(jax.random.fold_in(arg_keys[3], 71), 0),
        "branch": touch_ends((jax.random.randint(arg_keys[2], (NB,), 0, 2) < 1).astype(jnp.int32), jax.random.fold_in(arg_keys[2], 1), 0, 1),
    }


EXACT = lax.Precision.HIGHEST


def reference(blocks, columns, branch):
    slot_total = CGROUPS * SPG
    flat_cols = columns.reshape(NB, slot_total)
    flat_blocks = blocks.reshape(NB, slot_total, BS, BS)

    def one_row(row_id):
        own_cols = columns[row_id]
        inner_ids = flat_cols[row_id]
        far_blocks = blocks[inner_ids]
        far_cols = columns[inner_ids]
        matches = (far_cols[:, :, :, None] == own_cols[None, :, None, :]).astype(jnp.float32)
        chosen = jnp.einsum("sgbj,sgbxy->sgjxy", matches, far_blocks, precision=EXACT)
        return jnp.einsum("sxy,sgjyz->gjxz", flat_blocks[row_id], chosen, precision=EXACT)

    product = lax.map(one_row, jnp.arange(NB, dtype=jnp.int32))
    chooser = (branch == 1)[:, None, None, None, None]
    updated = jnp.where(chooser, product, 2.0 * blocks - product)
    row_ids = jnp.arange(NB, dtype=jnp.int32)[:, None, None]
    on_diag = (columns == row_ids).astype(jnp.float32)
    old_term = jnp.sum(on_diag * jnp.trace(blocks, axis1=3, axis2=4))
    new_term = jnp.sum(on_diag * jnp.trace(updated, axis1=3, axis2=4))
    return updated, jnp.stack([old_term, new_term])
```

```python
import functools

import jax
import jax.numpy as jnp
from jax import lax
from jax.experimental import pallas as pl
from jax.experimental.pallas import tpu as pltpu
from jax.sharding import PartitionSpec as P

BS = 128
SPG = 6


EXACT = lax.Precision.HIGHEST


def shifted(value, axis, steps):
    count = lax.axis_size(axis)
    pairs = [(source, (source + steps) % count) for source in range(count)]
    return lax.ppermute(value, axis, pairs)


def cannon_sum(a_blocks, a_cols, out_cols, moving, moving_cols, offset, panel, passer):
    grid_rows = lax.axis_size("row")
    my_row = lax.axis_index("row")
    out_count = a_blocks.shape[0]
    slot_total = a_blocks.shape[1] * a_blocks.shape[2]
    a_flat = a_blocks.reshape(out_count, slot_total, BS, BS)
    a_cflat = a_cols.reshape(out_count, slot_total)
    tile_rows = moving.shape[0]
    start_sum = jnp.zeros((out_count, SPG, BS, BS), jnp.float32)

    def contribute(running, pieces, piece_cols, step_index):
        source = (my_row - step_index) % grid_rows
        wanted = source * panel + offset + jnp.arange(tile_rows, dtype=jnp.int32)
        hits = (a_cflat[:, :, None] == wanted[None, None, :]).astype(jnp.float32)
        stacked = jnp.einsum("nst,nsxy->tnxy", hits, a_flat, precision=EXACT)
        matches = (piece_cols[:, None, None, :] == out_cols[None, :, :, None]).astype(jnp.float32)

        def one_tile_row(total, items):
            left_side, right_side, pairing = items
            products = jnp.einsum("nxy,byz->nbxz", left_side, right_side, precision=EXACT)
            return (total + jnp.einsum("njb,nbxz->njxz", pairing, products, precision=EXACT), 0)

        running, unused = lax.scan(one_tile_row, running, (stacked, pieces, matches))
        return running

    def turn(step_index, carry):
        running, pieces, piece_cols = carry
        running = contribute(running, pieces, piece_cols, step_index)
        pieces, piece_cols = passer(pieces, piece_cols)
        return (running, pieces, piece_cols)

    running, pieces, piece_cols = lax.fori_loop(
        0, grid_rows - 1, turn, (start_sum, moving, moving_cols)
    )
    return contribute(running, pieces, piece_cols, grid_rows - 1)


def pass_whole(pieces, piece_cols):
    return shifted((pieces, piece_cols), "row", 1)


def on_device(blocks, columns, branch):
    panel = blocks.shape[0]
    layer_count = lax.axis_size("depth")
    layer = lax.axis_index("depth")
    my_row = lax.axis_index("row")
    rows_half = panel // layer_count
    first_row = layer * rows_half
    own_blocks = blocks[:, 0]
    own_cols = columns[:, 0]
    half_blocks = lax.dynamic_slice_in_dim(blocks, first_row, rows_half, 0)
    half_cols = lax.dynamic_slice_in_dim(columns, first_row, rows_half, 0)
    a_blocks, a_cols = (
        lax.all_gather(half_blocks, "col", axis=1, tiled=True),
        lax.all_gather(half_cols, "col", axis=1, tiled=True),
    )
    partial_sum = cannon_sum(
        a_blocks, a_cols, half_cols[:, 0], own_blocks, own_cols, 0, panel, pass_whole
    )
    product = lax.all_gather(partial_sum, "depth", axis=0, tiled=True)
    chooser = (branch == 1)[:, None, None, None]
    updated = jnp.where(chooser, product, 2.0 * own_blocks - product)
    row_ids = my_row * panel + jnp.arange(panel, dtype=jnp.int32)
    on_diag = (own_cols == row_ids[:, None]).astype(jnp.float32)
    old_term = jnp.sum(on_diag * jnp.trace(own_blocks, axis1=2, axis2=3))
    new_term = jnp.sum(on_diag * jnp.trace(updated, axis1=2, axis2=3))
    traces = lax.psum(jnp.stack([old_term, new_term]), ("row", "col"))
    return (updated[:, None], traces)


MESH = pl.DeviceIdType.MESH
CHUNKS = 2


def place_kernel(cols_ref, blocks_ref, out_ref):
    row = pl.program_id(0)
    for slot in range(blocks_ref.shape[2]):
        at = lax.rem(cols_ref[row, slot], blocks_ref.shape[2])
        out_ref[:, pl.ds(pl.multiple_of(at * BS, BS), BS)] = blocks_ref[0, 0, slot]


def place(blocks, cols):
    panel, _, slots = blocks.shape[:3]
    return pl.pallas_call(
        place_kernel,
        grid_spec=pltpu.PrefetchScalarGridSpec(
            num_scalar_prefetch=1,
            grid=(panel,),
            in_specs=[pl.BlockSpec((1, 1, slots, BS, BS), lambda i, c: (i, 0, 0, 0, 0))],
            out_specs=pl.BlockSpec((BS, slots * BS), lambda i, c: (i, 0)),
        ),
        out_shape=jax.ShapeDtypeStruct((panel * BS, slots * BS), jnp.float32),
    )(cols, blocks)


def halves(value):
    high = value.astype(jnp.bfloat16)
    return high, (value - high.astype(jnp.float32)).astype(jnp.bfloat16)


def square_kernel(
    groups, cols_ref, branch_ref, tile, blocks_ref, out_ref, trace_ref,
    left, right, right_hi, right_lo, total, parts,
    z_send, z_recv, p_send, p_recv, sz_send, sz_recv, sp_send, sp_recv, t_send, t_recv,
):
    row, col, depth = lax.axis_index("row"), lax.axis_index("col"), lax.axis_index("depth")
    panel, slots = blocks_ref.shape[0], blocks_ref.shape[2]
    rows = tile.shape[0]
    half = rows // 2
    step = half // CHUNKS
    sibling = (row, col, 1 - depth)
    across = (row + 1 - 2 * (row % 2), (row + 2) % 4)
    corner = across[1] + 1 - 2 * (row % 2)

    barrier = pltpu.get_barrier_semaphore()

    def greet(peer, carry):
        @pl.when(peer != row * groups + col)
        def _():
            pl.semaphore_signal(
                barrier, inc=1, device_id=(peer // groups, peer % groups, depth), device_id_type=MESH
            )
        return carry

    pl.semaphore_signal(barrier, inc=1, device_id=sibling, device_id_type=MESH)
    lax.fori_loop(0, 4 * groups, greet, 0)
    pl.semaphore_wait(barrier, 4 * groups)

    def span(core, chunk):
        return pl.ds(pl.multiple_of(core * half + chunk * step, step), step)

    def copy(src, dst, send, recv, target):
        return pltpu.make_async_remote_copy(
            src_ref=src, dst_ref=dst, send_sem=send, recv_sem=recv, device_id=target, device_id_type=MESH
        )

    def z_source(side, hop):
        return col - hop if side == 0 else col + hop

    def z_has(side, hop):
        return col >= hop if side == 0 else col + hop < groups

    def z_goes(side, hop):
        ahead = col + 1 < groups if side == 0 else col >= 1
        if hop == 1:
            return ahead
        return jnp.logical_and(ahead, z_has(side, hop - 1))

    def z_copy(side, hop, chunk):
        source = z_source(side, hop - 1)
        at = span(depth, chunk)
        src = tile.at[at] if hop == 1 else left.at[source, at]
        target = (row, jnp.clip(col + 1, 0, groups - 1) if side == 0 else jnp.clip(col - 1, 0, groups - 1), depth)
        return copy(src, left.at[source, at], z_send.at[side, hop - 1, chunk], z_recv.at[side, hop - 1, chunk], target)

    def z_arrival(side, hop, chunk):
        place_at = left.at[z_source(side, hop), span(depth, chunk)]
        return copy(place_at, place_at, z_send.at[side, hop - 1, chunk], z_recv.at[side, hop - 1, chunk], sibling)

    def z_share(side, hop, chunk, core):
        place_at = left.at[z_source(side, hop), span(core, chunk)]
        return copy(place_at, place_at, sz_send.at[side, hop - 1, chunk], sz_recv.at[side, hop - 1, chunk], sibling)

    def z_take(hop, chunk):
        for side in range(2):
            @pl.when(z_has(side, hop))
            def _(side=side):
                z_arrival(side, hop, chunk).wait_recv()
                if hop + 1 < groups:
                    @pl.when(z_goes(side, hop + 1))
                    def _():
                        z_copy(side, hop + 1, chunk).start()
                z_share(side, hop, chunk, depth).start()

    def p_copy(axis, piece):
        target = (across[axis], col, depth)
        if piece < CHUNKS:
            at = span(depth, piece)
            src, dst = tile.at[at], right.at[row, at]
        else:
            at = span(depth, axis)
            src = dst = right.at[across[1 - axis], at]
        return copy(src, dst, p_send.at[axis, piece], p_recv.at[axis, piece], target)

    def p_place(axis, piece, core):
        if piece < CHUNKS:
            return right.at[across[axis], span(core, piece)]
        return right.at[corner, span(core, axis)]

    def p_arrival(axis, piece):
        place_at = p_place(axis, piece, depth)
        return copy(place_at, place_at, p_send.at[axis, piece], p_recv.at[axis, piece], sibling)

    def p_share(axis, piece, core):
        place_at = p_place(axis, piece, core)
        return copy(place_at, place_at, sp_send.at[axis, piece], sp_recv.at[axis, piece], sibling)

    for chunk in range(CHUNKS):
        for side in range(2):
            @pl.when(z_goes(side, 1))
            def _(side=side, chunk=chunk):
                z_copy(side, 1, chunk).start()
        for axis in range(2):
            p_copy(axis, chunk).start()

    block_rows = rows // 4

    def split_right(source, index):
        def some(part, carry):
            at = pl.ds(pl.multiple_of(part * block_rows, block_rows), block_rows)
            high, low = halves(source[at])
            right_hi[index, at] = high
            right_lo[index, at] = low
            return carry
        lax.fori_loop(0, 4, some, 0)

    def multiply(source, index, at, first=False):
        high, low = halves(source[at])
        dot = functools.partial(jnp.dot, preferred_element_type=jnp.float32)
        product = (dot(high, right_lo[index]) + dot(low, right_hi[index])) + dot(high, right_hi[index])
        for block in range(slots):
            piece = product[:, block * BS:(block + 1) * BS]
            total[block, at] = piece if first else total[block, at] + piece

    def multiply_all(source, index, first=False):
        def some(part, carry):
            multiply(source, index, pl.ds(pl.multiple_of(part * block_rows, block_rows), block_rows), first)
            return carry
        lax.fori_loop(0, 4, some, 0)

    split_right(tile, row)

    for chunk in range(CHUNKS):
        z_take(1, chunk)
        for axis in range(2):
            p_arrival(axis, chunk).wait_recv()
            if chunk == 1 - axis:
                p_copy(1 - axis, CHUNKS).start()
            p_share(axis, chunk, depth).start()
    for axis in range(2):
        for chunk in range(CHUNKS):
            p_share(axis, chunk, 1 - depth).wait_recv()
        split_right(right.at[across[axis]], across[axis])
    for axis in range(2):
        p_arrival(axis, CHUNKS).wait_recv()
        p_share(axis, CHUNKS, depth).start()
    for axis in range(2):
        p_share(axis, CHUNKS, 1 - depth).wait_recv()
    split_right(right.at[corner], corner)
    multiply_all(tile, col, True)

    def z_multiply(hop, chunk):
        for side in range(2):
            @pl.when(z_has(side, hop))
            def _(side=side):
                source = z_source(side, hop)
                multiply(left.at[source], source, span(depth, chunk))
                z_share(side, hop, chunk, 1 - depth).wait_recv()
                multiply(left.at[source], source, span(1 - depth, chunk))

    for hop in range(2, groups):
        for chunk in range(CHUNKS):
            z_take(hop, chunk)
            if (hop, chunk) == (2, 0):
                for early in range(CHUNKS):
                    z_multiply(1, early)
            z_multiply(hop, chunk)

    eye = lax.broadcasted_iota(jnp.int32, (BS, BS), 0) == lax.broadcasted_iota(jnp.int32, (BS, BS), 1)
    spot = lax.broadcasted_iota(jnp.int32, parts.shape[1:], 1)

    @pl.when(row == col)
    def _():
        old_sum = jnp.zeros((BS, BS), jnp.float32)
        new_sum = jnp.zeros((BS, BS), jnp.float32)
        for block in range(panel):
            at = pl.ds(block * BS, BS)
            old = tile[at, at]
            square = total[block, at]
            new = jnp.where(branch_ref[block] == 1, square, 2.0 * old - square)
            old_sum += jnp.where(eye, old, 0.0)
            new_sum += jnp.where(eye, new, 0.0)
        old_all, new_all = jnp.sum(old_sum), jnp.sum(new_sum)
        parts[row] = jnp.where(spot == 0, old_all, jnp.where(spot == 1, new_all, 0.0))

    def finish(block, carry):
        at = pl.ds(pl.multiple_of(block * BS, BS), BS)
        taken = branch_ref[block] == 1
        for slot in range(slots):
            square = total[lax.rem(cols_ref[block, slot], slots), at]
            out_ref[block, 0, slot] = jnp.where(taken, square, 2.0 * blocks_ref[block, 0, slot] - square)
        return carry

    lax.fori_loop(0, panel, finish, 0)

    def t_copy(peer):
        return copy(parts.at[row], parts.at[row], t_send.at[peer], t_recv.at[row], (peer // groups, peer % groups, depth))

    def to_peers(act):
        def one(peer, carry):
            @pl.when(peer != row * groups + col)
            def _():
                act(t_copy(peer))
            return carry
        lax.fori_loop(0, 4 * groups, one, 0)

    @pl.when(row == col)
    def _():
        to_peers(lambda c: c.start())

    for source in range(groups):
        @pl.when(jnp.logical_or(row != source, col != source))
        def _(source=source):
            copy(parts.at[source], parts.at[source], t_send.at[source], t_recv.at[source], sibling).wait_recv()
    sum_all = parts[0]
    for source in range(1, groups):
        sum_all = sum_all + parts[source]
    trace_ref[...] = sum_all

    @pl.when(row == col)
    def _():
        to_peers(lambda c: c.wait_send())

    for axis in range(2):
        for piece in range(CHUNKS + 1):
            p_copy(axis, piece).wait_send()
            p_share(axis, piece, depth).wait_send()
    for side in range(2):
        for hop in range(1, groups):
            for chunk in range(CHUNKS):
                @pl.when(z_goes(side, hop))
                def _(side=side, hop=hop, chunk=chunk):
                    z_copy(side, hop, chunk).wait_send()

                @pl.when(z_has(side, hop))
                def _(side=side, hop=hop, chunk=chunk):
                    z_share(side, hop, chunk, depth).wait_send()


def full_rows(groups, blocks, columns, branch):
    panel, _, slots = blocks.shape[:3]
    cols = columns[:, 0]
    tile = place(blocks, cols)
    size = panel * BS
    sems = pltpu.SemaphoreType.DMA
    vmem = pl.BlockSpec(memory_space=pltpu.VMEM)
    smem = pl.BlockSpec(memory_space=pltpu.SMEM)
    updated, traces = pl.pallas_call(
        functools.partial(square_kernel, groups),
        out_shape=(
            jax.ShapeDtypeStruct(blocks.shape, jnp.float32),
            jax.ShapeDtypeStruct((8, BS), jnp.float32),
        ),
        in_specs=[smem, smem, vmem, vmem],
        out_specs=(vmem, vmem),
        scratch_shapes=[
            pltpu.VMEM((groups, size, size), jnp.float32),
            pltpu.VMEM((groups, size, size), jnp.float32),
            pltpu.VMEM((groups, size, size), jnp.bfloat16),
            pltpu.VMEM((groups, size, size), jnp.bfloat16),
            pltpu.VMEM((slots, size, BS), jnp.float32),
            pltpu.VMEM((groups, 8, BS), jnp.float32),
            sems((2, groups - 1, CHUNKS)),
            sems((2, groups - 1, CHUNKS)),
            sems((2, CHUNKS + 1)),
            sems((2, CHUNKS + 1)),
            sems((2, groups - 1, CHUNKS)),
            sems((2, groups - 1, CHUNKS)),
            sems((2, CHUNKS + 1)),
            sems((2, CHUNKS + 1)),
            sems((4 * groups,)),
            sems((groups,)),
        ],
        compiler_params=pltpu.CompilerParams(
            collective_id=0, has_side_effects=True, vmem_limit_bytes=60 * 2**20
        ),
    )(cols, branch, tile, blocks)
    return updated, traces[0, :2]


def solution(mesh):
    placed = (P("row", "col", None, None, None), P("row", "col", None), P("row"))
    grid = mesh.shape["row"], mesh.shape["col"], mesh.shape["depth"]

    def per_device(blocks, columns, branch):
        panel, _, slots = blocks.shape[:3]
        if grid[0] == 4 and grid[1] == 4 and grid[2] == 2 and panel == slots:
            return full_rows(grid[1], blocks, columns, branch)
        return on_device(blocks, columns, branch)

    return jax.shard_map(
        per_device,
        mesh=mesh,
        in_specs=placed,
        out_specs=(P("row", "col", None, None, None), P()),
        check_vma=False,
    )
```

```python
import functools

import jax
import jax.numpy as jnp
from jax import lax
from jax.experimental import pallas as pl
from jax.experimental.pallas import tpu as pltpu
from jax.sharding import PartitionSpec as P

BS = 128
SPG = 6


EXACT = lax.Precision.HIGHEST


def shifted(value, axis, steps):
    count = lax.axis_size(axis)
    pairs = [(source, (source + steps) % count) for source in range(count)]
    return lax.ppermute(value, axis, pairs)


def cannon_sum(a_blocks, a_cols, out_cols, moving, moving_cols, offset, panel, passer):
    grid_rows = lax.axis_size("row")
    my_row = lax.axis_index("row")
    out_count = a_blocks.shape[0]
    slot_total = a_blocks.shape[1] * a_blocks.shape[2]
    a_flat = a_blocks.reshape(out_count, slot_total, BS, BS)
    a_cflat = a_cols.reshape(out_count, slot_total)
    tile_rows = moving.shape[0]
    start_sum = jnp.zeros((out_count, SPG, BS, BS), jnp.float32)

    def contribute(running, pieces, piece_cols, step_index):
        source = (my_row - step_index) % grid_rows
        wanted = source * panel + offset + jnp.arange(tile_rows, dtype=jnp.int32)
        hits = (a_cflat[:, :, None] == wanted[None, None, :]).astype(jnp.float32)
        stacked = jnp.einsum("nst,nsxy->tnxy", hits, a_flat, precision=EXACT)
        matches = (piece_cols[:, None, None, :] == out_cols[None, :, :, None]).astype(jnp.float32)

        def one_tile_row(total, items):
            left_side, right_side, pairing = items
            products = jnp.einsum("nxy,byz->nbxz", left_side, right_side, precision=EXACT)
            return (total + jnp.einsum("njb,nbxz->njxz", pairing, products, precision=EXACT), 0)

        running, unused = lax.scan(one_tile_row, running, (stacked, pieces, matches))
        return running

    def turn(step_index, carry):
        running, pieces, piece_cols = carry
        running = contribute(running, pieces, piece_cols, step_index)
        pieces, piece_cols = passer(pieces, piece_cols)
        return (running, pieces, piece_cols)

    running, pieces, piece_cols = lax.fori_loop(
        0, grid_rows - 1, turn, (start_sum, moving, moving_cols)
    )
    return contribute(running, pieces, piece_cols, grid_rows - 1)


def pass_whole(pieces, piece_cols):
    return shifted((pieces, piece_cols), "row", 1)


def on_device(blocks, columns, branch):
    panel = blocks.shape[0]
    layer_count = lax.axis_size("depth")
    layer = lax.axis_index("depth")
    my_row = lax.axis_index("row")
    rows_half = panel // layer_count
    first_row = layer * rows_half
    own_blocks = blocks[:, 0]
    own_cols = columns[:, 0]
    half_blocks = lax.dynamic_slice_in_dim(blocks, first_row, rows_half, 0)
    half_cols = lax.dynamic_slice_in_dim(columns, first_row, rows_half, 0)
    a_blocks, a_cols = (
        lax.all_gather(half_blocks, "col", axis=1, tiled=True),
        lax.all_gather(half_cols, "col", axis=1, tiled=True),
    )
    partial_sum = cannon_sum(
        a_blocks, a_cols, half_cols[:, 0], own_blocks, own_cols, 0, panel, pass_whole
    )
    product = lax.all_gather(partial_sum, "depth", axis=0, tiled=True)
    chooser = (branch == 1)[:, None, None, None]
    updated = jnp.where(chooser, product, 2.0 * own_blocks - product)
    row_ids = my_row * panel + jnp.arange(panel, dtype=jnp.int32)
    on_diag = (own_cols == row_ids[:, None]).astype(jnp.float32)
    old_term = jnp.sum(on_diag * jnp.trace(own_blocks, axis1=2, axis2=3))
    new_term = jnp.sum(on_diag * jnp.trace(updated, axis1=2, axis2=3))
    traces = lax.psum(jnp.stack([old_term, new_term]), ("row", "col"))
    return (updated[:, None], traces)


MESH = pl.DeviceIdType.MESH
CHUNKS = 2


def halves(value):
    high = value.astype(jnp.bfloat16)
    return high, (value - high.astype(jnp.float32)).astype(jnp.bfloat16)


def square_kernel(
    groups, cols_ref, branch_ref, blocks_hbm, out_ref, trace_ref,
    blocks_ref, tile, in_sem, left, right, right_hi, right_lo, total, parts,
    z_send, z_recv, p_send, p_recv, sz_send, sz_recv, sp_send, sp_recv, t_send, t_recv,
):
    row, col, depth = lax.axis_index("row"), lax.axis_index("col"), lax.axis_index("depth")
    panel, slots = blocks_ref.shape[:2]
    rows = tile.shape[0]
    half = rows // 2
    step = half // CHUNKS
    sibling = (row, col, 1 - depth)
    across = (row + 1 - 2 * (row % 2), (row + 2) % 4)
    corner = across[1] + 1 - 2 * (row % 2)

    barrier = pltpu.get_barrier_semaphore()

    def greet(peer, carry):
        @pl.when(peer != row * groups + col)
        def _():
            pl.semaphore_signal(
                barrier, inc=1, device_id=(peer // groups, peer % groups, depth), device_id_type=MESH
            )
        return carry

    pl.semaphore_signal(barrier, inc=1, device_id=sibling, device_id_type=MESH)
    lax.fori_loop(0, 4 * groups, greet, 0)

    per_half = panel // 2

    def ordered(block):
        at = pl.ds(pl.multiple_of(block * BS, BS), BS)
        for target_slot in range(slots):
            source = 0
            for slot in range(1, slots):
                source = jnp.where(lax.rem(cols_ref[block, 0, slot], slots) == target_slot, slot, source)
            tile[at, target_slot * BS:(target_slot + 1) * BS] = blocks_ref[block, source]

    def incoming(turn):
        block = lax.rem(depth * per_half + turn, panel)
        return block, pltpu.make_async_copy(blocks_hbm.at[block, 0], blocks_ref.at[block], in_sem.at[turn])

    for turn in range(panel):
        incoming(turn)[1].start()
    for turn in range(panel):
        incoming(turn)[1].wait()
    for turn in range(panel):
        ordered(incoming(turn)[0])
    pl.semaphore_wait(barrier, 4 * groups)

    def span(core, chunk):
        return pl.ds(pl.multiple_of(core * half + chunk * step, step), step)

    def copy(src, dst, send, recv, target):
        return pltpu.make_async_remote_copy(
            src_ref=src, dst_ref=dst, send_sem=send, recv_sem=recv, device_id=target, device_id_type=MESH
        )

    def z_source(side, hop):
        return col - hop if side == 0 else col + hop

    def z_has(side, hop):
        return col >= hop if side == 0 else col + hop < groups

    def z_goes(side, hop):
        ahead = col + 1 < groups if side == 0 else col >= 1
        if hop == 1:
            return ahead
        return jnp.logical_and(ahead, z_has(side, hop - 1))

    def z_copy(side, hop, chunk):
        source = z_source(side, hop - 1)
        at = span(depth, chunk)
        src = tile.at[at] if hop == 1 else left.at[source, at]
        target = (row, jnp.clip(col + 1, 0, groups - 1) if side == 0 else jnp.clip(col - 1, 0, groups - 1), depth)
        return copy(src, left.at[source, at], z_send.at[side, hop - 1, chunk], z_recv.at[side, hop - 1, chunk], target)

    def z_arrival(side, hop, chunk):
        place_at = left.at[z_source(side, hop), span(depth, chunk)]
        return copy(place_at, place_at, z_send.at[side, hop - 1, chunk], z_recv.at[side, hop - 1, chunk], sibling)

    def z_share(side, hop, chunk, core):
        place_at = left.at[z_source(side, hop), span(core, chunk)]
        return copy(place_at, place_at, sz_send.at[side, hop - 1, chunk], sz_recv.at[side, hop - 1, chunk], sibling)

    def z_take(hop, chunk):
        for side in range(2):
            @pl.when(z_has(side, hop))
            def _(side=side):
                z_arrival(side, hop, chunk).wait_recv()
                if hop + 1 < groups:
                    @pl.when(z_goes(side, hop + 1))
                    def _():
                        z_copy(side, hop + 1, chunk).start()
                z_share(side, hop, chunk, depth).start()

    def p_copy(axis, piece):
        target = (across[axis], col, depth)
        if piece < CHUNKS:
            at = span(depth, piece)
            src, dst = tile.at[at], right.at[row, at]
        else:
            at = span(depth, axis)
            src = dst = right.at[across[1 - axis], at]
        return copy(src, dst, p_send.at[axis, piece], p_recv.at[axis, piece], target)

    def p_place(axis, piece, core):
        if piece < CHUNKS:
            return right.at[across[axis], span(core, piece)]
        return right.at[corner, span(core, axis)]

    def p_arrival(axis, piece):
        place_at = p_place(axis, piece, depth)
        return copy(place_at, place_at, p_send.at[axis, piece], p_recv.at[axis, piece], sibling)

    def p_share(axis, piece, core):
        place_at = p_place(axis, piece, core)
        return copy(place_at, place_at, sp_send.at[axis, piece], sp_recv.at[axis, piece], sibling)

    for chunk in range(CHUNKS):
        for side in range(2):
            @pl.when(z_goes(side, 1))
            def _(side=side, chunk=chunk):
                z_copy(side, 1, chunk).start()
        for axis in range(2):
            p_copy(axis, chunk).start()

    block_rows = rows // 4

    def split_right(source, index):
        def some(part, carry):
            at = pl.ds(pl.multiple_of(part * block_rows, block_rows), block_rows)
            high, low = halves(source[at])
            right_hi[index, at] = high
            right_lo[index, at] = low
            return carry
        lax.fori_loop(0, 4, some, 0)

    def multiply(source, index, at, first=False):
        high, low = halves(source[at])
        dot = functools.partial(jnp.dot, preferred_element_type=jnp.float32)
        product = (dot(high, right_lo[index]) + dot(low, right_hi[index])) + dot(high, right_hi[index])
        for block in range(slots):
            piece = product[:, block * BS:(block + 1) * BS]
            total[block, at] = piece if first else total[block, at] + piece

    def multiply_all(source, index, first=False):
        def some(part, carry):
            multiply(source, index, pl.ds(pl.multiple_of(part * block_rows, block_rows), block_rows), first)
            return carry
        lax.fori_loop(0, 4, some, 0)

    split_right(tile, row)

    for chunk in range(CHUNKS):
        z_take(1, chunk)
        for axis in range(2):
            p_arrival(axis, chunk).wait_recv()
            if chunk == 1 - axis:
                p_copy(1 - axis, CHUNKS).start()
            p_share(axis, chunk, depth).start()
    for axis in range(2):
        for chunk in range(CHUNKS):
            p_share(axis, chunk, 1 - depth).wait_recv()
        split_right(right.at[across[axis]], across[axis])
    for axis in range(2):
        p_arrival(axis, CHUNKS).wait_recv()
        p_share(axis, CHUNKS, depth).start()
    for axis in range(2):
        p_share(axis, CHUNKS, 1 - depth).wait_recv()
    split_right(right.at[corner], corner)
    multiply_all(tile, col, True)

    def z_multiply(hop, chunk):
        for side in range(2):
            @pl.when(z_has(side, hop))
            def _(side=side):
                source = z_source(side, hop)
                multiply(left.at[source], source, span(depth, chunk))
                z_share(side, hop, chunk, 1 - depth).wait_recv()
                multiply(left.at[source], source, span(1 - depth, chunk))

    for hop in range(2, groups):
        for chunk in range(CHUNKS):
            z_take(hop, chunk)
            if (hop, chunk) == (2, 0):
                for early in range(CHUNKS):
                    z_multiply(1, early)
            z_multiply(hop, chunk)

    eye = lax.broadcasted_iota(jnp.int32, (BS, BS), 0) == lax.broadcasted_iota(jnp.int32, (BS, BS), 1)
    spot = lax.broadcasted_iota(jnp.int32, parts.shape[1:], 1)

    @pl.when(row == col)
    def _():
        old_sum = jnp.zeros((BS, BS), jnp.float32)
        new_sum = jnp.zeros((BS, BS), jnp.float32)
        for block in range(panel):
            at = pl.ds(block * BS, BS)
            old = tile[at, at]
            square = total[block, at]
            new = jnp.where(branch_ref[block] == 1, square, 2.0 * old - square)
            old_sum += jnp.where(eye, old, 0.0)
            new_sum += jnp.where(eye, new, 0.0)
        old_all, new_all = jnp.sum(old_sum), jnp.sum(new_sum)
        parts[row] = jnp.where(spot == 0, old_all, jnp.where(spot == 1, new_all, 0.0))

    def finish(block, carry):
        at = pl.ds(pl.multiple_of(block * BS, BS), BS)
        taken = branch_ref[block] == 1
        for slot in range(slots):
            square = total[lax.rem(cols_ref[block, 0, slot], slots), at]
            out_ref[block, 0, slot] = jnp.where(taken, square, 2.0 * blocks_ref[block, slot] - square)
        return carry

    def t_copy(peer):
        return copy(parts.at[row], parts.at[row], t_send.at[peer], t_recv.at[row], (peer // groups, peer % groups, depth))

    def to_peers(act):
        def one(peer, carry):
            @pl.when(peer != row * groups + col)
            def _():
                act(t_copy(peer))
            return carry
        lax.fori_loop(0, 4 * groups, one, 0)

    lax.fori_loop(0, panel, finish, 0)

    @pl.when(row == col)
    def _():
        to_peers(lambda c: c.start())

    for source in range(groups):
        @pl.when(jnp.logical_or(row != source, col != source))
        def _(source=source):
            copy(parts.at[source], parts.at[source], t_send.at[source], t_recv.at[source], sibling).wait_recv()
    sum_all = parts[0]
    for source in range(1, groups):
        sum_all = sum_all + parts[source]
    trace_ref[...] = sum_all

    @pl.when(row == col)
    def _():
        to_peers(lambda c: c.wait_send())

    for axis in range(2):
        for piece in range(CHUNKS + 1):
            p_copy(axis, piece).wait_send()
            p_share(axis, piece, depth).wait_send()
    for side in range(2):
        for hop in range(1, groups):
            for chunk in range(CHUNKS):
                @pl.when(z_goes(side, hop))
                def _(side=side, hop=hop, chunk=chunk):
                    z_copy(side, hop, chunk).wait_send()

                @pl.when(z_has(side, hop))
                def _(side=side, hop=hop, chunk=chunk):
                    z_share(side, hop, chunk, depth).wait_send()


def full_rows(groups, blocks, columns, branch):
    panel, _, slots = blocks.shape[:3]
    size = panel * BS
    sems = pltpu.SemaphoreType.DMA
    vmem = pl.BlockSpec(memory_space=pltpu.VMEM)
    smem = pl.BlockSpec(memory_space=pltpu.SMEM)
    updated, traces = pl.pallas_call(
        functools.partial(square_kernel, groups),
        out_shape=(
            pltpu.VMEM(blocks.shape, jnp.float32),
            jax.ShapeDtypeStruct((8, BS), jnp.float32),
        ),
        in_specs=[smem, smem, pl.BlockSpec(memory_space=pl.ANY)],
        out_specs=(vmem, vmem),
        scratch_shapes=[
            pltpu.VMEM((panel, slots, BS, BS), jnp.float32),
            pltpu.VMEM((size, size), jnp.float32),
            sems((panel,)),
            pltpu.VMEM((groups, size, size), jnp.float32),
            pltpu.VMEM((groups, size, size), jnp.float32),
            pltpu.VMEM((groups, size, size), jnp.bfloat16),
            pltpu.VMEM((groups, size, size), jnp.bfloat16),
            pltpu.VMEM((slots, size, BS), jnp.float32),
            pltpu.VMEM((groups, 8, BS), jnp.float32),
            sems((2, groups - 1, CHUNKS)),
            sems((2, groups - 1, CHUNKS)),
            sems((2, CHUNKS + 1)),
            sems((2, CHUNKS + 1)),
            sems((2, groups - 1, CHUNKS)),
            sems((2, groups - 1, CHUNKS)),
            sems((2, CHUNKS + 1)),
            sems((2, CHUNKS + 1)),
            sems((4 * groups,)),
            sems((groups,)),
        ],
        compiler_params=pltpu.CompilerParams(
            collective_id=0, has_side_effects=True, vmem_limit_bytes=60 * 2**20
        ),
    )(columns, branch, blocks)
    return updated, traces[0, :2]


def solution(mesh):
    placed = (P("row", "col", None, None, None), P("row", "col", None), P("row"))
    grid = mesh.shape["row"], mesh.shape["col"], mesh.shape["depth"]

    def per_device(blocks, columns, branch):
        panel, _, slots = blocks.shape[:3]
        if grid[0] == 4 and grid[1] == 4 and grid[2] == 2 and panel == slots:
            return full_rows(grid[1], blocks, columns, branch)
        return on_device(blocks, columns, branch)

    return jax.shard_map(
        per_device,
        mesh=mesh,
        in_specs=placed,
        out_specs=(P("row", "col", None, None, None), P()),
        check_vma=False,
    )
```

```python
import functools

import jax
import jax.numpy as jnp
from jax import lax
from jax.experimental import pallas as pl
from jax.experimental.pallas import tpu as pltpu
from jax.sharding import PartitionSpec as P

BS = 128
SPG = 6


EXACT = lax.Precision.HIGHEST


def shifted(value, axis, steps):
    count = lax.axis_size(axis)
    pairs = [(source, (source + steps) % count) for source in range(count)]
    return lax.ppermute(value, axis, pairs)


def cannon_sum(a_blocks, a_cols, out_cols, moving, moving_cols, offset, panel, passer):
    grid_rows = lax.axis_size("row")
    my_row = lax.axis_index("row")
    out_count = a_blocks.shape[0]
    slot_total = a_blocks.shape[1] * a_blocks.shape[2]
    a_flat = a_blocks.reshape(out_count, slot_total, BS, BS)
    a_cflat = a_cols.reshape(out_count, slot_total)
    tile_rows = moving.shape[0]
    start_sum = jnp.zeros((out_count, SPG, BS, BS), jnp.float32)

    def contribute(running, pieces, piece_cols, step_index):
        source = (my_row - step_index) % grid_rows
        wanted = source * panel + offset + jnp.arange(tile_rows, dtype=jnp.int32)
        hits = (a_cflat[:, :, None] == wanted[None, None, :]).astype(jnp.float32)
        stacked = jnp.einsum("nst,nsxy->tnxy", hits, a_flat, precision=EXACT)
        matches = (piece_cols[:, None, None, :] == out_cols[None, :, :, None]).astype(jnp.float32)

        def one_tile_row(total, items):
            left_side, right_side, pairing = items
            products = jnp.einsum("nxy,byz->nbxz", left_side, right_side, precision=EXACT)
            return (total + jnp.einsum("njb,nbxz->njxz", pairing, products, precision=EXACT), 0)

        running, unused = lax.scan(one_tile_row, running, (stacked, pieces, matches))
        return running

    def turn(step_index, carry):
        running, pieces, piece_cols = carry
        running = contribute(running, pieces, piece_cols, step_index)
        pieces, piece_cols = passer(pieces, piece_cols)
        return (running, pieces, piece_cols)

    running, pieces, piece_cols = lax.fori_loop(
        0, grid_rows - 1, turn, (start_sum, moving, moving_cols)
    )
    return contribute(running, pieces, piece_cols, grid_rows - 1)


def pass_whole(pieces, piece_cols):
    return shifted((pieces, piece_cols), "row", 1)


def on_device(blocks, columns, branch):
    panel = blocks.shape[0]
    layer_count = lax.axis_size("depth")
    layer = lax.axis_index("depth")
    my_row = lax.axis_index("row")
    rows_half = panel // layer_count
    first_row = layer * rows_half
    own_blocks = blocks[:, 0]
    own_cols = columns[:, 0]
    half_blocks = lax.dynamic_slice_in_dim(blocks, first_row, rows_half, 0)
    half_cols = lax.dynamic_slice_in_dim(columns, first_row, rows_half, 0)
    a_blocks, a_cols = (
        lax.all_gather(half_blocks, "col", axis=1, tiled=True),
        lax.all_gather(half_cols, "col", axis=1, tiled=True),
    )
    partial_sum = cannon_sum(
        a_blocks, a_cols, half_cols[:, 0], own_blocks, own_cols, 0, panel, pass_whole
    )
    product = lax.all_gather(partial_sum, "depth", axis=0, tiled=True)
    chooser = (branch == 1)[:, None, None, None]
    updated = jnp.where(chooser, product, 2.0 * own_blocks - product)
    row_ids = my_row * panel + jnp.arange(panel, dtype=jnp.int32)
    on_diag = (own_cols == row_ids[:, None]).astype(jnp.float32)
    old_term = jnp.sum(on_diag * jnp.trace(own_blocks, axis1=2, axis2=3))
    new_term = jnp.sum(on_diag * jnp.trace(updated, axis1=2, axis2=3))
    traces = lax.psum(jnp.stack([old_term, new_term]), ("row", "col"))
    return (updated[:, None], traces)


MESH = pl.DeviceIdType.MESH
CHUNKS = 2


def halves(value):
    high = value.astype(jnp.bfloat16)
    return high, (value - high.astype(jnp.float32)).astype(jnp.bfloat16)


def square_kernel(
    groups, cols_ref, branch_ref, blocks_hbm, out_ref, trace_ref,
    blocks_ref, tile, in_sem, left, right, right_hi, right_lo, total, turned, diagonal, parts,
    z_send, z_recv, p_send, p_recv, sz_send, sz_recv, sp_send, sp_recv, t_send, t_recv,
):
    row, col, depth = lax.axis_index("row"), lax.axis_index("col"), lax.axis_index("depth")
    panel, slots = blocks_ref.shape[:2]
    rows = tile.shape[0]
    half = rows // 2
    step = half // CHUNKS
    sibling = (row, col, 1 - depth)
    across = (row + 1 - 2 * (row % 2), (row + 2) % 4)
    corner = across[1] + 1 - 2 * (row % 2)

    barrier = pltpu.get_barrier_semaphore()

    def greet(peer, carry):
        @pl.when(peer != row * groups + col)
        def _():
            pl.semaphore_signal(
                barrier, inc=1, device_id=(peer // groups, peer % groups, depth), device_id_type=MESH
            )
        return carry

    pl.semaphore_signal(barrier, inc=1, device_id=sibling, device_id_type=MESH)
    lax.fori_loop(0, 4 * groups, greet, 0)

    per_half = panel // 2

    def ordered(block):
        at = pl.ds(pl.multiple_of(block * BS, BS), BS)
        for target_slot in range(slots):
            source = 0
            for slot in range(1, slots):
                source = jnp.where(lax.rem(cols_ref[block, 0, slot], slots) == target_slot, slot, source)
            tile[at, target_slot * BS:(target_slot + 1) * BS] = blocks_ref[block, source]

    def incoming(turn):
        block = lax.rem(depth * per_half + turn, panel)
        return block, pltpu.make_async_copy(blocks_hbm.at[block, 0], blocks_ref.at[block], in_sem.at[turn])

    for turn in range(panel):
        incoming(turn)[1].start()
    for turn in range(panel):
        incoming(turn)[1].wait()
    for turn in range(panel):
        ordered(incoming(turn)[0])
    pl.semaphore_wait(barrier, 4 * groups)

    def span(core, chunk):
        return pl.ds(pl.multiple_of(core * half + chunk * step, step), step)

    def copy(src, dst, send, recv, target):
        return pltpu.make_async_remote_copy(
            src_ref=src, dst_ref=dst, send_sem=send, recv_sem=recv, device_id=target, device_id_type=MESH
        )

    def z_source(side, hop):
        return col - hop if side == 0 else col + hop

    def z_has(side, hop):
        return col >= hop if side == 0 else col + hop < groups

    def z_goes(side, hop):
        ahead = col + 1 < groups if side == 0 else col >= 1
        if hop == 1:
            return ahead
        return jnp.logical_and(ahead, z_has(side, hop - 1))

    def z_copy(side, hop, chunk):
        source = z_source(side, hop - 1)
        at = span(depth, chunk)
        src = tile.at[at] if hop == 1 else left.at[source, at]
        target = (row, jnp.clip(col + 1, 0, groups - 1) if side == 0 else jnp.clip(col - 1, 0, groups - 1), depth)
        return copy(src, left.at[source, at], z_send.at[side, hop - 1, chunk], z_recv.at[side, hop - 1, chunk], target)

    def z_arrival(side, hop, chunk):
        place_at = left.at[z_source(side, hop), span(depth, chunk)]
        return copy(place_at, place_at, z_send.at[side, hop - 1, chunk], z_recv.at[side, hop - 1, chunk], sibling)

    def z_share(side, hop, chunk, core):
        place_at = left.at[z_source(side, hop), span(core, chunk)]
        return copy(place_at, place_at, sz_send.at[side, hop - 1, chunk], sz_recv.at[side, hop - 1, chunk], sibling)

    def z_take(hop, chunk):
        for side in range(2):
            @pl.when(z_has(side, hop))
            def _(side=side):
                z_arrival(side, hop, chunk).wait_recv()
                if hop + 1 < groups:
                    @pl.when(z_goes(side, hop + 1))
                    def _():
                        z_copy(side, hop + 1, chunk).start()
                z_share(side, hop, chunk, depth).start()

    def p_copy(axis, piece):
        target = (across[axis], col, depth)
        if piece < CHUNKS:
            at = span(depth, piece)
            src, dst = tile.at[at], right.at[row, at]
        else:
            at = span(depth, axis)
            src = dst = right.at[across[1 - axis], at]
        return copy(src, dst, p_send.at[axis, piece], p_recv.at[axis, piece], target)

    def p_place(axis, piece, core):
        if piece < CHUNKS:
            return right.at[across[axis], span(core, piece)]
        return right.at[corner, span(core, axis)]

    def p_arrival(axis, piece):
        place_at = p_place(axis, piece, depth)
        return copy(place_at, place_at, p_send.at[axis, piece], p_recv.at[axis, piece], sibling)

    def p_share(axis, piece, core):
        place_at = p_place(axis, piece, core)
        return copy(place_at, place_at, sp_send.at[axis, piece], sp_recv.at[axis, piece], sibling)

    for chunk in range(CHUNKS):
        for side in range(2):
            @pl.when(z_goes(side, 1))
            def _(side=side, chunk=chunk):
                z_copy(side, 1, chunk).start()
        for axis in range(2):
            p_copy(axis, chunk).start()

    block_rows = rows // 4

    def split_right(source, index):
        def some(part, carry):
            at = pl.ds(pl.multiple_of(part * block_rows, block_rows), block_rows)
            high, low = halves(source[at])
            right_hi[index, at] = high
            right_lo[index, at] = low
            return carry
        lax.fori_loop(0, 4, some, 0)

    def multiply(source, index, at, first=False):
        high, low = halves(source[at])
        dot = functools.partial(jnp.dot, preferred_element_type=jnp.float32)
        product = (dot(high, right_lo[index]) + dot(low, right_hi[index])) + dot(high, right_hi[index])
        for block in range(slots):
            piece = product[:, block * BS:(block + 1) * BS]
            total[block, at] = piece if first else total[block, at] + piece

        @pl.when(row == col)
        def _():
            few = 32

            def some(part, carry):
                far = pl.ds(pl.multiple_of(at.start + part * few, few), few)
                terms = source[far] * turned[index, far]
                line = terms[:, :BS]
                for block in range(1, slots):
                    line = line + terms[:, block * BS:(block + 1) * BS]
                diagonal[far] = line if first else diagonal[far] + line
                return carry

            lax.fori_loop(0, at.size // few, some, 0)

    def multiply_all(source, index, first=False):
        def some(part, carry):
            multiply(source, index, pl.ds(pl.multiple_of(part * block_rows, block_rows), block_rows), first)
            return carry
        lax.fori_loop(0, 4, some, 0)

    split_right(tile, row)

    for chunk in range(CHUNKS):
        z_take(1, chunk)
        for axis in range(2):
            p_arrival(axis, chunk).wait_recv()
            if chunk == 1 - axis:
                p_copy(1 - axis, CHUNKS).start()
            p_share(axis, chunk, depth).start()
    for axis in range(2):
        for chunk in range(CHUNKS):
            p_share(axis, chunk, 1 - depth).wait_recv()
        split_right(right.at[across[axis]], across[axis])
    for axis in range(2):
        p_arrival(axis, CHUNKS).wait_recv()
        p_share(axis, CHUNKS, depth).start()
    for axis in range(2):
        p_share(axis, CHUNKS, 1 - depth).wait_recv()
    split_right(right.at[corner], corner)

    @pl.when(row == col)
    def _():
        def turn(source, index):
            def some(block, carry):
                at = pl.ds(pl.multiple_of(block * BS, BS), BS)
                for other in range(slots):
                    turned[index, at, other * BS:(other + 1) * BS] = source[other * BS:(other + 1) * BS, at].T
                return carry
            lax.fori_loop(0, panel, some, 0)

        turn(tile, row)
        for index in (across[0], across[1], corner):
            turn(right.at[index], index)

    multiply_all(tile, col, True)

    def z_multiply(hop, chunk):
        for side in range(2):
            @pl.when(z_has(side, hop))
            def _(side=side):
                source = z_source(side, hop)
                multiply(left.at[source], source, span(depth, chunk))
                z_share(side, hop, chunk, 1 - depth).wait_recv()
                multiply(left.at[source], source, span(1 - depth, chunk))

    for hop in range(2, groups):
        for chunk in range(CHUNKS):
            z_take(hop, chunk)
            if (hop, chunk) == (2, 0):
                for early in range(CHUNKS):
                    z_multiply(1, early)
            z_multiply(hop, chunk)

    eye = lax.broadcasted_iota(jnp.int32, (BS, BS), 0) == lax.broadcasted_iota(jnp.int32, (BS, BS), 1)
    spot = lax.broadcasted_iota(jnp.int32, parts.shape[1:], 1)

    @pl.when(row == col)
    def _():
        old_sum = jnp.zeros((BS, BS), jnp.float32)
        new_sum = jnp.zeros((BS, BS), jnp.float32)
        for block in range(panel):
            at = pl.ds(block * BS, BS)
            old = jnp.where(eye, tile[at, at], 0.0)
            square = diagonal[at]
            old_sum += old
            new_sum += jnp.where(branch_ref[block] == 1, square, 2.0 * old - square)
        old_all, new_all = jnp.sum(old_sum), jnp.sum(new_sum)
        parts[row] = jnp.where(spot == 0, old_all, jnp.where(spot == 1, new_all, 0.0))

    def finish(block, carry):
        at = pl.ds(pl.multiple_of(block * BS, BS), BS)
        taken = branch_ref[block] == 1
        for slot in range(slots):
            square = total[lax.rem(cols_ref[block, 0, slot], slots), at]
            out_ref[block, 0, slot] = jnp.where(taken, square, 2.0 * blocks_ref[block, slot] - square)
        return carry

    def t_copy(peer):
        return copy(parts.at[row], parts.at[row], t_send.at[peer], t_recv.at[row], (peer // groups, peer % groups, depth))

    def to_peers(act):
        def one(peer, carry):
            @pl.when(peer != row * groups + col)
            def _():
                act(t_copy(peer))
            return carry
        lax.fori_loop(0, 4 * groups, one, 0)

    lax.fori_loop(0, panel, finish, 0)

    @pl.when(row == col)
    def _():
        to_peers(lambda c: c.start())

    for source in range(groups):
        @pl.when(jnp.logical_or(row != source, col != source))
        def _(source=source):
            copy(parts.at[source], parts.at[source], t_send.at[source], t_recv.at[source], sibling).wait_recv()
    sum_all = parts[0]
    for source in range(1, groups):
        sum_all = sum_all + parts[source]
    trace_ref[...] = sum_all

    @pl.when(row == col)
    def _():
        to_peers(lambda c: c.wait_send())

    for axis in range(2):
        for piece in range(CHUNKS + 1):
            p_copy(axis, piece).wait_send()
            p_share(axis, piece, depth).wait_send()
    for side in range(2):
        for hop in range(1, groups):
            for chunk in range(CHUNKS):
                @pl.when(z_goes(side, hop))
                def _(side=side, hop=hop, chunk=chunk):
                    z_copy(side, hop, chunk).wait_send()

                @pl.when(z_has(side, hop))
                def _(side=side, hop=hop, chunk=chunk):
                    z_share(side, hop, chunk, depth).wait_send()


def full_rows(groups, blocks, columns, branch):
    panel, _, slots = blocks.shape[:3]
    size = panel * BS
    sems = pltpu.SemaphoreType.DMA
    vmem = pl.BlockSpec(memory_space=pltpu.VMEM)
    smem = pl.BlockSpec(memory_space=pltpu.SMEM)
    updated, traces = pl.pallas_call(
        functools.partial(square_kernel, groups),
        out_shape=(
            pltpu.VMEM(blocks.shape, jnp.float32),
            jax.ShapeDtypeStruct((8, BS), jnp.float32),
        ),
        in_specs=[smem, smem, pl.BlockSpec(memory_space=pl.ANY)],
        out_specs=(vmem, vmem),
        scratch_shapes=[
            pltpu.VMEM((panel, slots, BS, BS), jnp.float32),
            pltpu.VMEM((size, size), jnp.float32),
            sems((panel,)),
            pltpu.VMEM((groups, size, size), jnp.float32),
            pltpu.VMEM((groups, size, size), jnp.float32),
            pltpu.VMEM((groups, size, size), jnp.bfloat16),
            pltpu.VMEM((groups, size, size), jnp.bfloat16),
            pltpu.VMEM((slots, size, BS), jnp.float32),
            pltpu.VMEM((groups, size, size), jnp.float32),
            pltpu.VMEM((size, BS), jnp.float32),
            pltpu.VMEM((groups, 8, BS), jnp.float32),
            sems((2, groups - 1, CHUNKS)),
            sems((2, groups - 1, CHUNKS)),
            sems((2, CHUNKS + 1)),
            sems((2, CHUNKS + 1)),
            sems((2, groups - 1, CHUNKS)),
            sems((2, groups - 1, CHUNKS)),
            sems((2, CHUNKS + 1)),
            sems((2, CHUNKS + 1)),
            sems((4 * groups,)),
            sems((groups,)),
        ],
        compiler_params=pltpu.CompilerParams(
            collective_id=0, has_side_effects=True, vmem_limit_bytes=60 * 2**20
        ),
    )(columns, branch, blocks)
    return updated, traces[0, :2]


def solution(mesh):
    placed = (P("row", "col", None, None, None), P("row", "col", None), P("row"))
    grid = mesh.shape["row"], mesh.shape["col"], mesh.shape["depth"]

    def per_device(blocks, columns, branch):
        panel, _, slots = blocks.shape[:3]
        if grid[0] == 4 and grid[1] == 4 and grid[2] == 2 and panel == slots:
            return full_rows(grid[1], blocks, columns, branch)
        return on_device(blocks, columns, branch)

    return jax.shard_map(
        per_device,
        mesh=mesh,
        in_specs=placed,
        out_specs=(P("row", "col", None, None, None), P()),
        check_vma=False,
    )
```
